32 devices in a mesh: gx: 4 (over z), gy: 8 (over y, x, core).
Axes of the slice: x: 2, y: 2, z: 4, core: 2. Of those that a mesh axis runs over, the one named last changes fastest.
Arguments:
- conductivity: float32 [128, 256, 128], P('gx', 'gy'), may hold values from 0.25 to 4
- source: float32 [128, 256, 128], P('gx', 'gy'), may hold values from -12 to 12
- initial: float32 [128, 256, 128], P('gx', 'gy'), may hold values from -3 to 3
Outputs:
- solution: float32 [128, 256, 128], P('gx', 'gy')
The draws below stay inside these ranges and needn't reach their ends.
All inputs are finite; a program needn't handle non-finite values.
Results may differ from the reference program's by a relative error of at most 0.0003.
Values sent between devices are 32-bit elements; how exact they have to be, the bound alone decides.
A program may use at most 64 MiB of HBM per device.

```python
import math
import jax
import jax.numpy as jnp
from jax import lax

BS = 16
NU = 3
CG_ITERS = 32
NX = 128
NY = 256
NZ = 128
N_GX = 4
N_GY = 8


def draw_source(key, part):
    return 4.0 * jax.random.truncated_normal(key, -3.0, 3.0, (NX, NY, NZ), jnp.float32)


def level_of(key, dims, split, smallest, high):
    def one(dim, blocks):
        heights = jax.random.uniform(jax.random.fold_in(jax.random.fold_in(key, 6), dim), (blocks,), jnp.float32, smallest / len(split), high / len(split))
        return jnp.repeat(jnp.exp(heights), dims[dim] // blocks).reshape((-1,) + (1,) * (len(dims) - dim - 1))

    level = one(*split[0])
    for cut in split[1:]:
        level = level * one(*cut)
    return level


def bell_draw(own_key, dims, spread, reach, shards=(), kind=jnp.bfloat16):
    values = jax.random.normal(own_key, dims, jnp.float32) * spread
    if len(shards) > 0:
        values = level_of(own_key, dims, shards, -0.22, 0.18) * values
    return jnp.clip(values, min=-reach, max=reach).astype(kind)


def setup_inputs(seed: int = 0) -> dict:
    seeds = jax.random.split(jax.random.key(seed), 4)
    return {
        "conductivity": jnp.clip(jnp.exp(math.log(4.0) - 2.7725887 * jax.random.uniform(seeds[0], (NX, NY, NZ), jnp.float32) ** level_of(seeds[0], (NX, NY, NZ), ((0, 4), (1, 8)), -0.2, 0.2)), 0.25, 4.0),
        "source": draw_source(jax.random.fold_in(seeds[3], 71), 0),
        "initial": bell_draw(seeds[2], (NX, NY, NZ), 0.5, 3.0, ((0, 4), (1, 8)), jnp.float32),
    }


relax_weight = 0.8


def operate(padded, cond_pad):
    center_cond = cond_pad[1:-1, 1:-1]
    center = padded[1:-1, 1:-1]
    face_east = 0.5 * (center_cond + cond_pad[2:, 1:-1])
    face_west = 0.5 * (center_cond + cond_pad[:-2, 1:-1])
    face_north = 0.5 * (center_cond + cond_pad[1:-1, 2:])
    face_south = 0.5 * (center_cond + cond_pad[1:-1, :-2])
    between = 0.5 * (center_cond[:, :, 1:] + center_cond[:, :, :-1])
    zero_plane = jnp.zeros(center.shape[:2] + (1,), center.dtype)
    face_up = jnp.concatenate([between, zero_plane], 2)
    face_down = jnp.concatenate([zero_plane, between], 2)
    value_up = jnp.concatenate([center[:, :, 1:], zero_plane], 2)
    value_down = jnp.concatenate([zero_plane, center[:, :, :-1]], 2)
    diagonal = face_east + face_west + face_north + face_south + face_up + face_down
    neighbor_sum = (face_east * padded[2:, 1:-1] + face_west * padded[:-2, 1:-1]
                    + face_north * padded[1:-1, 2:] + face_south * padded[1:-1, :-2]
                    + face_up * value_up + face_down * value_down)
    return diagonal * center - neighbor_sum, diagonal, center_cond, center


def smooth_once(padded, cond_pad, source):
    applied, diagonal, center_cond, center = operate(padded, cond_pad)
    inside = center_cond > 0
    update = relax_weight * (source - applied) / jnp.where(inside, diagonal, 1.0)
    return jnp.where(inside, center + update, 0.0)


def coarse_apply(estimate, coarse_diag, flow_east, flow_north):
    edge_rows = jnp.zeros((1, estimate.shape[1]), estimate.dtype)
    edge_cols = jnp.zeros((estimate.shape[0], 1), estimate.dtype)
    ahead_x = jnp.concatenate([estimate[1:], edge_rows], 0)
    carried_x = flow_east * estimate
    behind_x = jnp.concatenate([edge_rows, carried_x[:-1]], 0)
    ahead_y = jnp.concatenate([estimate[:, 1:], edge_cols], 1)
    carried_y = flow_north * estimate
    behind_y = jnp.concatenate([edge_cols, carried_y[:, :-1]], 1)
    return coarse_diag * estimate - flow_east * ahead_x - behind_x - flow_north * ahead_y - behind_y


def coarse_solve(coarse_source, coarse_diag, flow_east, flow_north):
    def iterate_once(counter, carried):
        estimate, remainder, search, norm_now = carried
        product = coarse_apply(search, coarse_diag, flow_east, flow_north)
        alpha_step = norm_now / jnp.sum(search * product)
        estimate = estimate + alpha_step * search
        remainder = remainder - alpha_step * product
        norm_next = jnp.sum(remainder * remainder)
        search = remainder + (norm_next / norm_now) * search
        return estimate, remainder, search, norm_next

    start_state = (jnp.zeros_like(coarse_source), coarse_source, coarse_source,
                   jnp.sum(coarse_source * coarse_source))
    return lax.fori_loop(0, CG_ITERS, iterate_once, start_state)[0]


def reference(conductivity, source, initial):
    extent_x = 2 * BS
    extent_y = 2 * BS
    margins = ((1, 1), (1, 1), (0, 0))
    cond_pad = jnp.pad(conductivity, margins)
    starts = jnp.arange(N_GX, dtype=jnp.int32) * extent_x

    def sweep_all(iterate):
        padded = jnp.pad(iterate, margins)

        def one_slab(offset):
            return smooth_once(lax.dynamic_slice_in_dim(padded, offset, extent_x + 2, 0),
                               lax.dynamic_slice_in_dim(cond_pad, offset, extent_x + 2, 0),
                               lax.dynamic_slice_in_dim(source, offset, extent_x, 0))

        return lax.map(one_slab, starts).reshape(conductivity.shape)

    iterate = initial
    for repeat in range(NU):
        iterate = sweep_all(iterate)
    padded = jnp.pad(iterate, margins)

    def slab_residual(offset):
        applied = operate(lax.dynamic_slice_in_dim(padded, offset, extent_x + 2, 0),
                          lax.dynamic_slice_in_dim(cond_pad, offset, extent_x + 2, 0))[0]
        remainder = lax.dynamic_slice_in_dim(source, offset, extent_x, 0) - applied
        return jnp.sum(remainder.reshape(extent_x, N_GY, extent_y, -1), axis=(0, 2, 3))

    coarse_source = lax.map(slab_residual, starts)
    whole_x = conductivity.shape[0]
    high_x = jnp.pad(conductivity, ((0, 1), (0, 0), (0, 0)))
    plane = 0.5 * (conductivity[extent_x - 1::extent_x] + high_x[extent_x::extent_x])
    flow_east = jnp.sum(plane.reshape(N_GX, N_GY, extent_y, -1), axis=(2, 3))
    low_x = jnp.pad(conductivity, ((1, 0), (0, 0), (0, 0)))
    plane = 0.5 * (conductivity[0::extent_x] + low_x[0:whole_x:extent_x])
    flow_west = jnp.sum(plane.reshape(N_GX, N_GY, extent_y, -1), axis=(2, 3))
    high_y = jnp.pad(conductivity, ((0, 0), (0, 1), (0, 0)))
    plane = 0.5 * (conductivity[:, extent_y - 1::extent_y] + high_y[:, extent_y::extent_y])
    flow_north = jnp.sum(plane.reshape(N_GX, extent_x, N_GY, -1), axis=(1, 3))
    low_y = jnp.pad(conductivity, ((0, 0), (1, 0), (0, 0)))
    plane = 0.5 * (conductivity[:, 0::extent_y] + low_y[:, 0:conductivity.shape[1]:extent_y])
    flow_south = jnp.sum(plane.reshape(N_GX, extent_x, N_GY, -1), axis=(1, 3))
    coarse_diag = flow_east + flow_west + flow_north + flow_south
    correction = coarse_solve(coarse_source, coarse_diag, flow_east, flow_north)
    iterate = iterate + jnp.repeat(jnp.repeat(correction, extent_x, 0), extent_y, 1)[:, :, None]
    for repeat in range(NU):
        iterate = sweep_all(iterate)
    return iterate
```

```python
import functools

import jax
import jax.numpy as jnp
from jax import lax
from jax.experimental import pallas as pl
from jax.experimental.pallas import tpu as pltpu
from jax.sharding import PartitionSpec as P

NU = 3
CG_ITERS = 32
H = NU + 1

relax_weight = 0.8
MESH = pl.DeviceIdType.MESH
DIRS = [(1, 0), (-1, 0), (0, 1), (0, -1), (1, 1), (1, -1), (-1, 1), (-1, -1)]


def inside(ix, iy, cx, cy):
    return (ix >= 0) & (ix < cx) & (iy >= 0) & (iy < cy)


def rows_loop(lo, hi, step, carry):
    count = hi - lo
    pairs = count // 2

    def two(i, c):
        x = lo + 2 * i
        return step(x + 1, step(x, c))

    carry = lax.fori_loop(0, pairs, two, carry)
    if count % 2:
        carry = step(hi - 1, carry)
    return carry


def kernel(cx, cy, nx, ny, *refs):
    (k_in, f_in, u_in, k4, f4, u4, out,
     K, F, U, V, CE, CN, CU, W, YLO, YHI,
     XLO2, XHI2, YLO2, YHI2, PLO, PHI, GC, GS, E,
     lsem, osem, ssem, rsem, ssem2, rsem2,
     c1s, c1r, c2s, c2r, s1s, s1r, s2s, s2r) = refs
    X = nx + 2 * H
    Y = ny + 2 * H
    ix = lax.axis_index("gx")
    iy = lax.axis_index("gy")
    full = [k_in, f_in, u_in]
    quad = [k4, f4, u4]
    ext = [K, F, U]

    barrier = pltpu.get_barrier_semaphore()

    def greet_x(k, c):
        pl.semaphore_signal(barrier, inc=1, device_id=(lax.rem(ix + k, cx), iy), device_id_type=MESH)
        return c

    def greet_y(k, c):
        pl.semaphore_signal(barrier, inc=1, device_id=(ix, lax.rem(iy + k, cy)), device_id_type=MESH)
        return c

    lax.fori_loop(1, cx, greet_x, 0)
    lax.fori_loop(1, cy, greet_y, 0)
    for dx, dy in DIRS[4:]:
        @pl.when(inside(ix + dx, iy + dy, cx, cy))
        def _(dx=dx, dy=dy):
            pl.semaphore_signal(barrier, inc=1, device_id=(ix + dx, iy + dy), device_id_type=MESH)

    local = [pltpu.make_async_copy(full[a], ext[a].at[H:H + nx, 0:ny, :], lsem.at[a]) for a in range(3)]
    for copy in local:
        copy.start()

    sides_x = (ix > 0).astype(jnp.int32) + (ix < cx - 1).astype(jnp.int32)
    sides_y = (iy > 0).astype(jnp.int32) + (iy < cy - 1).astype(jnp.int32)
    pl.semaphore_wait(barrier, (cx - 1) + (cy - 1) + sides_x * sides_y)

    def halo(a, d):
        dx, dy = DIRS[d]
        slot = a * 8 + d
        src_rows = {1: (nx - H, nx), -1: (0, H), 0: (0, nx)}[dx]
        dst_rows = {1: (0, H), -1: (X - H, X), 0: (H, H + nx)}[dx]
        if dy == 0:
            src = full[a].at[src_rows[0]:src_rows[1]]
            dst = ext[a].at[dst_rows[0]:dst_rows[1], 0:ny, :]
        else:
            src = quad[a].at[src_rows[0]:src_rows[1], ny // H - 1 if dy == 1 else 0]
            dst = (YLO if dy == 1 else YHI).at[a, dst_rows[0]:dst_rows[1]]
        return pltpu.make_async_remote_copy(
            src_ref=src, dst_ref=dst, send_sem=ssem.at[slot], recv_sem=rsem.at[slot],
            device_id=(ix + dx, iy + dy), device_id_type=MESH)

    def each(d, sign, act):
        dx, dy = DIRS[d]
        pl.when(inside(ix + sign * dx, iy + sign * dy, cx, cy))(act)

    for d in range(8):
        def start(d=d):
            for a in range(3):
                halo(a, d).start()
        each(d, 1, start)

    def clear_when_absent(d):
        dx, dy = DIRS[d]
        rows = {1: (0, H), -1: (X - H, X), 0: (H, H + nx)}[dx]

        @pl.when(jnp.logical_not(inside(ix - dx, iy - dy, cx, cy)))
        def _():
            if dy == 0:
                for a in range(3):
                    ext[a][rows[0]:rows[1], 0:ny, :] = jnp.zeros((H, ny, 128), jnp.float32)
                (XLO2 if dx == 1 else XHI2)[...] = jnp.zeros((NU, ny, 128), jnp.float32)
            else:
                wide = YLO if dy == 1 else YHI
                wide2 = YLO2 if dy == 1 else YHI2
                for a in range(3):
                    wide[a, rows[0]:rows[1]] = jnp.zeros((rows[1] - rows[0], H, 128), jnp.float32)
                wide2[rows[0]:rows[1]] = jnp.zeros((rows[1] - rows[0], H, 128), jnp.float32)

    for d in range(8):
        clear_when_absent(d)

    for copy in local:
        copy.wait()

    f_total = rows_loop(H, H + nx, lambda x, c: c + F[x, 0:ny, :], jnp.zeros((ny, 128), jnp.float32))

    for d in range(8):
        def finish(d=d):
            for a in range(3):
                halo(a, d).wait_recv()
        each(d, -1, finish)

    def unpack(x, c):
        for a in range(3):
            ext[a][x, ny:ny + H, :] = YHI[a, x]
            ext[a][x, ny + H:Y, :] = YLO[a, x]
        return c

    rows_loop(0, X, unpack, 0)

    lane = lax.broadcasted_iota(jnp.int32, (Y, 128), 1)
    up_half = jnp.where(lane < 127, 0.5, 0.0)

    def next_y(v):
        return pltpu.roll(v, Y - 1, 0)

    def last_y(v):
        return pltpu.roll(v, 1, 0)

    def next_z(v):
        return pltpu.roll(v, 127, 1)

    def last_z(v):
        return pltpu.roll(v, 1, 1)

    def faces(x, c):
        k, west, total = c
        k_next = K[x + 1]
        east = 0.5 * (k + k_next)
        north = 0.5 * (k + next_y(k))
        up = up_half * (k + next_z(k))
        d = east + west + north + last_y(north) + up + last_z(up)
        CE[x] = east
        CN[x] = north
        CU[x] = up
        W[x] = jnp.where(k > 0, relax_weight / jnp.where(k > 0, d, 1.0), 0.0)
        return k_next, east, total + north

    k1 = K[1]
    first = 0.5 * (K[0] + k1)
    CE[0] = first
    zero = jnp.zeros((Y, 128), jnp.float32)
    carry = rows_loop(1, H, faces, (k1, first, zero))
    carry = rows_loop(H, H + nx, faces, (carry[0], carry[1], zero))
    north_total = carry[2]
    rows_loop(H + nx, X - 1, faces, carry)

    def whole_sum(v):
        return jnp.sum(jnp.sum(v, axis=0, keepdims=True), axis=1, keepdims=True)

    flow_e = whole_sum(CE[X - H - 1, 0:ny, :])
    flow_w = whole_sum(CE[H - 1, 0:ny, :])
    flow_n = whole_sum(north_total[ny - 1:ny])
    flow_s = whole_sum(north_total[Y - 1:Y])
    coarse_diag = flow_e + flow_w + flow_n + flow_s
    GC[iy, ix, 0:1, :] = jnp.broadcast_to(coarse_diag, (1, 128))
    GC[iy, ix, 1:2, :] = jnp.broadcast_to(flow_e, (1, 128))
    GC[iy, ix, 2:3, :] = jnp.broadcast_to(flow_n, (1, 128))
    GC[iy, ix, 3:4, :] = jnp.zeros((1, 128), jnp.float32)

    def along_x(G, ss, rs):
        def of(k):
            return pltpu.make_async_remote_copy(
                src_ref=G.at[iy, ix], dst_ref=G.at[iy, ix], send_sem=ss.at[k - 1], recv_sem=rs.at[k - 1],
                device_id=(lax.rem(ix + k, cx), iy), device_id_type=MESH)
        return of

    def along_y(G, ss, rs):
        def of(k):
            return pltpu.make_async_remote_copy(
                src_ref=G.at[iy], dst_ref=G.at[iy], send_sem=ss.at[k - 1], recv_sem=rs.at[k - 1],
                device_id=(ix, lax.rem(iy + k, cy)), device_id_type=MESH)
        return of

    def run(of, count, method):
        def go(k, c):
            getattr(of(k), method)()
            return c
        lax.fori_loop(1, count, go, 0)

    coef_x, coef_y = along_x(GC, c1s, c1r), along_y(GC, c2s, c2r)
    sum_x, sum_y = along_x(GS, s1s, s1r), along_y(GS, s2s, s2r)
    run(coef_x, cx, "start")

    def sweep(src, dst, lo, hi, final=None):
        def step(x, c):
            u, west, total = c
            u_next = src[x + 1]
            east = CE[x] * (u_next - u)
            cn = CN[x]
            north = cn * (next_y(u) - u)
            up = CU[x] * (next_z(u) - u)
            change = (east - west) + (north - last_y(north)) + (up - last_z(up))
            new = u + W[x] * (F[x] + change)
            dst[x] = new
            if final is not None:
                total = total + cn * (next_y(new) - new)
            return u_next, east, total
        u = src[lo]
        west = CE[lo - 1] * (u - src[lo - 1])
        zero = jnp.zeros((Y, 128), jnp.float32) if final is not None else 0
        if final is None:
            rows_loop(lo, hi, step, (u, west, zero))
            return None
        carry = rows_loop(lo, final[0], step, (u, west, zero))
        carry = rows_loop(final[0], final[1], step, (carry[0], carry[1], zero))
        rows_loop(final[1], hi, step, carry)
        return carry[2]

    sweep(U, V, 1, X - 1)
    run(coef_x, cx, "wait_recv")
    run(coef_y, cy, "start")
    sweep(V, U, 2, X - 2)
    y_total = sweep(U, V, 3, X - 3, (H, H + nx))

    low, high = H - 1, X - H - 1
    x_total = (CE[high, 0:ny, :] * (V[high + 1, 0:ny, :] - V[high, 0:ny, :])
               - CE[low, 0:ny, :] * (V[low + 1, 0:ny, :] - V[low, 0:ny, :]))
    per_lane = (jnp.sum(f_total + x_total, axis=0, keepdims=True)
                + (y_total[ny - 1:ny] - y_total[Y - 1:Y]))
    GS[iy, ix] = jnp.broadcast_to(jnp.sum(per_lane, axis=1, keepdims=True), (1, 128))
    run(sum_x, cx, "start")

    def pack(x, c):
        PLO[x] = V[H + x, 0:H, :]
        PHI[x] = V[H + x, ny - H:ny, :]
        return c

    rows_loop(0, nx, pack, 0)

    def halo2(d):
        dx, dy = DIRS[d]
        src_rows = {1: (nx - H, nx), -1: (0, H), 0: (0, nx)}[dx]
        dst_rows = {1: (0, H), -1: (X - H, X), 0: (H, H + nx)}[dx]
        if dy == 0:
            src = V.at[nx + 1:nx + H, 0:ny, :] if dx == 1 else V.at[H:H + NU, 0:ny, :]
            dst = XLO2 if dx == 1 else XHI2
        else:
            src = (PHI if dy == 1 else PLO).at[src_rows[0]:src_rows[1]]
            dst = (YLO2 if dy == 1 else YHI2).at[dst_rows[0]:dst_rows[1]]
        return pltpu.make_async_remote_copy(
            src_ref=src, dst_ref=dst, send_sem=ssem2.at[d], recv_sem=rsem2.at[d],
            device_id=(ix + dx, iy + dy), device_id_type=MESH)

    for d in range(8):
        each(d, 1, lambda d=d: halo2(d).start())

    run(coef_y, cy, "wait_recv")
    row_y = lax.broadcasted_iota(jnp.int32, (cy, 128), 0)
    diag = [GC[:, x, 0, :] for x in range(cx)]
    east = [GC[:, x, 1, :] for x in range(cx - 1)]
    north = [jnp.where(row_y < cy - 1, GC[:, x, 2, :], 0.0) for x in range(cx)]
    south = [pltpu.roll(n, 1, 0) for n in north]

    run(sum_x, cx, "wait_recv")
    run(sum_y, cy, "start")
    run(sum_y, cy, "wait_recv")
    coarse_source = [GS[:, x, 0, :] for x in range(cx)]

    def dot(a, b):
        total = a[0] * b[0]
        for x in range(1, cx):
            total = total + a[x] * b[x]
        return jnp.sum(total, axis=0, keepdims=True)

    def coarse_apply(p):
        product = []
        for x in range(cx):
            v = diag[x] * p[x] - north[x] * pltpu.roll(p[x], cy - 1, 0) - south[x] * pltpu.roll(p[x], 1, 0)
            if x < cx - 1:
                v = v - east[x] * p[x + 1]
            if x > 0:
                v = v - east[x - 1] * p[x - 1]
            product.append(v)
        return product

    def iterate_once(counter, carried):
        estimate, remainder, search, norm_now = carried
        product = coarse_apply(search)
        alpha = norm_now / dot(search, product)
        estimate = [e + alpha * s for e, s in zip(estimate, search)]
        remainder = [r - alpha * q for r, q in zip(remainder, product)]
        norm_next = dot(remainder, remainder)
        beta = norm_next / norm_now
        search = [r + beta * s for r, s in zip(remainder, search)]
        return estimate, remainder, search, norm_next

    state = ([jnp.zeros((cy, 128), jnp.float32)] * cx, coarse_source, coarse_source,
             dot(coarse_source, coarse_source))
    estimate = lax.fori_loop(0, CG_ITERS, iterate_once, state)[0]
    for x in range(cx):
        E[x] = estimate[x]

    ring = lax.broadcasted_iota(jnp.int32, (Y, 128), 0)

    def share(dx):
        def one(dy):
            jx, jy = ix + dx, iy + dy
            row = E[jnp.clip(jx, 0, cx - 1), pl.ds(jnp.clip(jy, 0, cy - 1), 1), :]
            keep = inside(jx, jy, cx, cy).astype(jnp.float32)
            return jnp.broadcast_to(row * keep, (Y, 128))
        return jnp.where(ring < ny, one(0), jnp.where(ring < ny + H, one(1), one(-1)))

    shares = {dx: share(dx) for dx in (-1, 0, 1)}

    for d in range(8):
        each(d, -1, lambda d=d: halo2(d).wait_recv())
    for d in range(8):
        each(d, 1, lambda d=d: halo2(d).wait_send())

    def edge(x, dx):
        V[x, ny:ny + H, :] = YHI2[x]
        V[x, ny + H:Y, :] = YLO2[x]
        V[x] = V[x] + shares[dx]

    for i in range(NU):
        V[1 + i, 0:ny, :] = XLO2[i]
        V[X - H + i, 0:ny, :] = XHI2[i]
    for i in range(NU):
        edge(1 + i, -1)
        edge(X - H + i, 1)

    def middle(x, c):
        edge(x, 0)
        return c

    rows_loop(H, H + nx, middle, 0)

    sweep(V, U, 2, X - 2)
    sweep(U, V, 3, X - 3)
    sweep(V, U, 4, X - 4)
    back = pltpu.make_async_copy(U.at[H:H + nx, 0:ny, :], out, osem)
    back.start()

    for d in range(8):
        def sent(d=d):
            for a in range(3):
                halo(a, d).wait_send()
        each(d, 1, sent)
    run(coef_x, cx, "wait_send")
    run(coef_y, cy, "wait_send")
    run(sum_x, cx, "wait_send")
    run(sum_y, cy, "wait_send")
    back.wait()


def body(conductivity, source, initial):
    nx, ny, nz = conductivity.shape
    cx, cy = lax.axis_size("gx"), lax.axis_size("gy")
    X, Y = nx + 2 * H, ny + 2 * H
    args = (conductivity, source, initial)
    quads = tuple(a.reshape(nx, ny // H, H, nz) for a in args)
    wide = pltpu.VMEM((X, Y, nz), jnp.float32)
    dma = pltpu.SemaphoreType.DMA

    def vmem(*shape):
        return pltpu.VMEM(shape, jnp.float32)

    return pl.pallas_call(
        functools.partial(kernel, cx, cy, nx, ny),
        out_shape=jax.ShapeDtypeStruct((nx, ny, nz), jnp.float32),
        in_specs=[pl.BlockSpec(memory_space=pl.ANY)] * 6,
        out_specs=pl.BlockSpec(memory_space=pl.ANY),
        scratch_shapes=[wide] * 8 + [
            vmem(3, X, H, nz), vmem(3, X, H, nz),
            vmem(NU, ny, nz), vmem(NU, ny, nz), vmem(X, H, nz), vmem(X, H, nz),
            vmem(nx, H, nz), vmem(nx, H, nz),
            vmem(cy, cx, 4, nz), vmem(cy, cx, 1, nz), vmem(cx, cy, nz),
            dma((3,)), dma,
            dma((24,)), dma((24,)), dma((8,)), dma((8,)),
            dma((cx - 1,)), dma((cx - 1,)), dma((cy - 1,)), dma((cy - 1,)),
            dma((cx - 1,)), dma((cx - 1,)), dma((cy - 1,)), dma((cy - 1,)),
        ],
        compiler_params=pltpu.CompilerParams(collective_id=0, has_side_effects=True),
        name="cycle",
    )(*args, *quads)


def solution(mesh):
    return jax.shard_map(
        body,
        mesh=mesh,
        in_specs=(P("gx", "gy", None), P("gx", "gy", None), P("gx", "gy", None)),
        out_specs=P("gx", "gy", None),
        check_vma=False,
    )
```

```python
import functools

import jax
import jax.numpy as jnp
from jax import lax
from jax.experimental import pallas as pl
from jax.experimental.pallas import tpu as pltpu
from jax.sharding import PartitionSpec as P

NU = 3
CG_ITERS = 32
H = NU + 1
WIDTH = (NU, NU - 1, NU)

relax_weight = 0.8
MESH = pl.DeviceIdType.MESH
DIRS = [(1, 0), (-1, 0), (0, 1), (0, -1), (1, 1), (1, -1), (-1, 1), (-1, -1)]


def inside(ix, iy, cx, cy):
    return (ix >= 0) & (ix < cx) & (iy >= 0) & (iy < cy)


def rows_loop(lo, hi, step, carry):
    count = hi - lo
    pairs = count // 2

    def two(i, c):
        x = lo + 2 * i
        return step(x + 1, step(x, c))

    carry = lax.fori_loop(0, pairs, two, carry)
    if count % 2:
        carry = step(hi - 1, carry)
    return carry


ROWS = 8


def blocks_loop(lo, hi, block, carry):
    count = (hi - lo) // ROWS
    carry = lax.fori_loop(0, count, lambda i, c: block(lo + ROWS * i, c, ROWS), carry)
    if (hi - lo) % ROWS:
        carry = block(lo + ROWS * count, carry, (hi - lo) % ROWS)
    return carry


def kernel(cx, cy, nx, ny, *refs):
    (k_in, f_in, u_in, k1, f1, u1, out,
     K, F, U, V, CE, CN, CU, CD, W, YLO_K, YLO_F, YLO_U, YHI_K, YHI_F, YHI_U,
     XLO2, XHI2, YLO2, YHI2, PLO, PHI, GC, GS, E, R,
     lsem, osem, ssem, rsem, ssem2, rsem2,
     c1s, c1r, c2s, c2r, s1s, s1r, s2s, s2r) = refs
    X = nx + 2 * H
    Y = ny + 2 * H
    ix = lax.axis_index("gx")
    iy = lax.axis_index("gy")
    full = [k_in, f_in, u_in]
    thin = [k1, f1, u1]
    ext = [K, F, U]
    YLO = [YLO_K, YLO_F, YLO_U]
    YHI = [YHI_K, YHI_F, YHI_U]

    barrier = pltpu.get_barrier_semaphore()

    def greet_x(k, c):
        pl.semaphore_signal(barrier, inc=1, device_id=(lax.rem(ix + k, cx), iy), device_id_type=MESH)
        return c

    def greet_y(k, c):
        pl.semaphore_signal(barrier, inc=1, device_id=(ix, lax.rem(iy + k, cy)), device_id_type=MESH)
        return c

    lax.fori_loop(1, cx, greet_x, 0)
    lax.fori_loop(1, cy, greet_y, 0)
    for dx, dy in DIRS[4:]:
        @pl.when(inside(ix + dx, iy + dy, cx, cy))
        def _(dx=dx, dy=dy):
            pl.semaphore_signal(barrier, inc=1, device_id=(ix + dx, iy + dy), device_id_type=MESH)

    local = [pltpu.make_async_copy(full[a], ext[a].at[H:H + nx, 0:ny, :], lsem.at[a]) for a in range(3)]
    for copy in local:
        copy.start()

    sides_x = (ix > 0).astype(jnp.int32) + (ix < cx - 1).astype(jnp.int32)
    sides_y = (iy > 0).astype(jnp.int32) + (iy < cy - 1).astype(jnp.int32)
    pl.semaphore_wait(barrier, (cx - 1) + (cy - 1) + sides_x * sides_y)

    def spans(dx, w):
        src = {1: (nx - w, nx), -1: (0, w), 0: (0, nx)}[dx]
        dst = {1: (H - w, H), -1: (X - H, X - H + w), 0: (H, H + nx)}[dx]
        return src, dst

    def halo(a, d):
        dx, dy = DIRS[d]
        slot = a * 8 + d
        w = WIDTH[a]
        src_rows, dst_rows = spans(dx, w)
        if dy == 0:
            src = full[a].at[src_rows[0]:src_rows[1]]
            dst = ext[a].at[dst_rows[0]:dst_rows[1], 0:ny, :]
        else:
            cols = (ny - w, ny) if dy == 1 else (0, w)
            src = thin[a].at[src_rows[0]:src_rows[1], cols[0]:cols[1]]
            dst = (YLO if dy == 1 else YHI)[a].at[dst_rows[0]:dst_rows[1]]
        return pltpu.make_async_remote_copy(
            src_ref=src, dst_ref=dst, send_sem=ssem.at[slot], recv_sem=rsem.at[slot],
            device_id=(ix + dx, iy + dy), device_id_type=MESH)

    def each(d, sign, act):
        dx, dy = DIRS[d]
        pl.when(inside(ix + sign * dx, iy + sign * dy, cx, cy))(act)

    for d in range(8):
        def start(d=d):
            for a in range(3):
                halo(a, d).start()
        each(d, 1, start)

    def clear_when_absent(d):
        dx, dy = DIRS[d]

        @pl.when(jnp.logical_not(inside(ix - dx, iy - dy, cx, cy)))
        def _():
            for a in range(3):
                w = WIDTH[a]
                lo, hi = spans(dx, w)[1]
                if dy == 0:
                    ext[a][lo:hi, 0:ny, :] = jnp.zeros((w, ny, 128), jnp.float32)
                else:
                    (YLO if dy == 1 else YHI)[a][lo:hi] = jnp.zeros((hi - lo, w, 1, 128), jnp.float32)
            if dy == 0:
                (XLO2 if dx == 1 else XHI2)[...] = jnp.zeros((NU, ny, 128), jnp.float32)
            else:
                lo, hi = spans(dx, H)[1]
                (YLO2 if dy == 1 else YHI2)[lo:hi] = jnp.zeros((hi - lo, H, 128), jnp.float32)

    for d in range(8):
        clear_when_absent(d)

    for copy in local:
        copy.wait()

    def along_x(G, ss, rs):
        def of(k):
            return pltpu.make_async_remote_copy(
                src_ref=G.at[iy, ix], dst_ref=G.at[iy, ix], send_sem=ss.at[k - 1], recv_sem=rs.at[k - 1],
                device_id=(lax.rem(ix + k, cx), iy), device_id_type=MESH)
        return of

    def along_y(G, ss, rs):
        def of(k):
            return pltpu.make_async_remote_copy(
                src_ref=G.at[iy], dst_ref=G.at[iy], send_sem=ss.at[k - 1], recv_sem=rs.at[k - 1],
                device_id=(ix, lax.rem(iy + k, cy)), device_id_type=MESH)
        return of

    def run(of, count, method):
        def go(k, c):
            getattr(of(k), method)()
            return c
        lax.fori_loop(1, count, go, 0)

    coef_x, coef_y = along_x(GC, c1s, c1r), along_y(GC, c2s, c2r)
    sum_x, sum_y = along_x(GS, s1s, s1r), along_y(GS, s2s, s2r)

    lane_row = lax.broadcasted_iota(jnp.int32, (1, 128), 1)

    def whole(v):
        return jnp.sum(jnp.sum(v, axis=0, keepdims=True), axis=1, keepdims=True)

    def in_lanes(values):
        row = jnp.zeros((1, 128), jnp.float32)
        for k, v in enumerate(values):
            row = jnp.where(lane_row == k, v, row)
        return row

    def outer(x, c):
        return c[0] + K[x, 0:1, :], c[1] + K[x, ny - 1:ny, :]

    none = jnp.zeros((1, 128), jnp.float32)
    y_first, y_last = rows_loop(H, H + nx, outer, (none, none))
    GC[iy, ix] = in_lanes([whole(K[H, 0:ny, :]), whole(K[H + nx - 1, 0:ny, :]), whole(y_first), whole(y_last)])
    run(coef_x, cx, "start")
    f_total = rows_loop(H, H + nx, lambda x, c: c + F[x, 0:ny, :], jnp.zeros((ny, 128), jnp.float32))
    f_total = jnp.sum(f_total, axis=0, keepdims=True)

    run(coef_x, cx, "wait_recv")
    run(coef_y, cy, "start")

    for d in range(8):
        def finish(d=d):
            for a in range(3):
                halo(a, d).wait_recv()
        each(d, -1, finish)

    def unpack(x, c):
        for a in range(3):
            w = WIDTH[a]
            ext[a][x, ny:ny + w, :] = YHI[a][x, :, 0, :]
            ext[a][x, Y - w:Y, :] = YLO[a][x, :, 0, :]
        return c

    rows_loop(1, X - 1, unpack, 0)

    lane = lax.broadcasted_iota(jnp.int32, (Y, 128), 1)
    up_half = jnp.where(lane < 127, 0.5, 0.0)
    down_half = jnp.where(lane > 0, 0.5, 0.0)

    def next_y(v):
        return pltpu.roll(v, Y - 1, 0)

    def last_y(v):
        return pltpu.roll(v, 1, 0)

    def next_z(v):
        return pltpu.roll(v, 127, 1)

    def last_z(v):
        return pltpu.roll(v, 1, 1)

    def faces(x, c, rows):
        k, west = c
        ks = [k] + [K[x + 1 + r] for r in range(rows)]
        ups = [next_z(ks[r]) for r in range(rows)]
        downs = [last_z(ks[r]) for r in range(rows)]
        for r in range(rows):
            k = ks[r]
            east = 0.5 * (k + ks[r + 1])
            north = 0.5 * (k + next_y(k))
            up = up_half * (k + ups[r])
            down = down_half * (k + downs[r])
            d = east + west + north + last_y(north) + up + down
            CE[x + r] = east
            CN[x + r] = north
            CU[x + r] = up
            CD[x + r] = down
            W[x + r] = jnp.where(k > 0, relax_weight / jnp.where(k > 0, d, 1.0), 0.0)
            west = east
        return ks[rows], west

    zero = jnp.zeros((Y, 128), jnp.float32)
    CE[1] = 0.5 * (K[1] + K[2])
    blocks_loop(2, X - 2, faces, (K[2], CE[1]))

    def sweep(src, dst, lo, hi, final=False):
        def block(x, c, rows):
            u, west, low, high = c
            us = [u] + [src[x + 1 + r] for r in range(rows)]
            ups = [next_z(us[r]) for r in range(rows)]
            downs = [last_z(us[r]) for r in range(rows)]
            for r in range(rows):
                u = us[r]
                east = CE[x + r] * (us[r + 1] - u)
                cn = CN[x + r]
                north = cn * (next_y(u) - u)
                change = ((east - west) + (north - last_y(north))
                          + (CU[x + r] * (ups[r] - u) + CD[x + r] * (downs[r] - u)))
                new = u + W[x + r] * (F[x + r] + change)
                dst[x + r] = new
                if final:
                    low, high = low + cn[Y - 1:Y] * new[0:1], high + cn[ny - 1:ny] * new[ny - 1:ny]
                west = east
            return us[rows], west, low, high

        start = (src[lo], CE[lo - 1] * (src[lo] - src[lo - 1]))
        start += (none, none) if final else (0, 0)
        return blocks_loop(lo, hi, block, start)[2:]

    sweep(U, V, 2, X - 2)
    sweep(V, U, 3, X - 3)
    y_low, y_high = sweep(U, V, 4, X - 4, True)

    x_low = jnp.sum(CE[H - 1, 0:ny, :] * V[H, 0:ny, :], axis=0, keepdims=True)
    x_high = jnp.sum(CE[X - H - 1, 0:ny, :] * V[X - H - 1, 0:ny, :], axis=0, keepdims=True)
    own = f_total - x_low - x_high - y_low - y_high
    GS[iy, ix] = in_lanes([jnp.sum(v, axis=1, keepdims=True) for v in (own, x_low, x_high, y_low, y_high)])
    run(sum_x, cx, "start")

    def pack(x, c):
        PLO[x] = V[H + x, 0:H, :]
        PHI[x] = V[H + x, ny - H:ny, :]
        return c

    rows_loop(0, nx, pack, 0)

    def halo2(d):
        dx, dy = DIRS[d]
        src_rows = {1: (nx - H, nx), -1: (0, H), 0: (0, nx)}[dx]
        dst_rows = {1: (0, H), -1: (X - H, X), 0: (H, H + nx)}[dx]
        if dy == 0:
            src = V.at[nx + 1:nx + H, 0:ny, :] if dx == 1 else V.at[H:H + NU, 0:ny, :]
            dst = XLO2 if dx == 1 else XHI2
        else:
            src = (PHI if dy == 1 else PLO).at[src_rows[0]:src_rows[1]]
            dst = (YLO2 if dy == 1 else YHI2).at[dst_rows[0]:dst_rows[1]]
        return pltpu.make_async_remote_copy(
            src_ref=src, dst_ref=dst, send_sem=ssem2.at[d], recv_sem=rsem2.at[d],
            device_id=(ix + dx, iy + dy), device_id_type=MESH)

    run(coef_y, cy, "wait_recv")
    row_y = lax.broadcasted_iota(jnp.int32, (cy, 128), 0)

    def tidy(G, k):
        for x in range(cx):
            for y in range(cy):
                R[k, x, y:y + 1, :] = G[y, x]
        return [R[k, x] for x in range(cx)]

    def lane_of(rows, k):
        return [jnp.broadcast_to(r[:, k:k + 1], (cy, 128)) for r in rows]

    def after_y(v):
        return jnp.where(row_y < cy - 1, pltpu.roll(v, cy - 1, 0), 0.0)

    def before_y(v):
        return jnp.where(row_y > 0, pltpu.roll(v, 1, 0), 0.0)

    coarse_rows = tidy(GC, 0)
    nil = jnp.zeros((cy, 128), jnp.float32)
    x_first, x_last, y_first, y_last = [lane_of(coarse_rows, k) for k in range(4)]
    east = [0.5 * (a + b) for a, b in zip(x_last, x_first[1:] + [nil])]
    west = [0.5 * (a + b) for a, b in zip(x_first, [nil] + x_last[:-1])]
    north = [0.5 * (a + after_y(b)) for a, b in zip(y_last, y_first)]
    south = [0.5 * (a + before_y(b)) for a, b in zip(y_first, y_last)]
    diag = [a + b + c + d for a, b, c, d in zip(east, west, north, south)]
    north = [jnp.where(row_y < cy - 1, n, 0.0) for n in north]
    south = [pltpu.roll(n, 1, 0) for n in north]

    run(sum_x, cx, "wait_recv")
    run(sum_y, cy, "start")
    for d in range(8):
        each(d, 1, lambda d=d: halo2(d).start())

    run(sum_y, cy, "wait_recv")
    coarse_rows = tidy(GS, 1)
    own, x_low, x_high, y_low, y_high = [lane_of(coarse_rows, k) for k in range(5)]
    coarse_source = [
        (a + after_y(b)) + (before_y(c) + d + e)
        for a, b, c, d, e in zip(own, y_low, y_high, x_low[1:] + [nil], [nil] + x_high[:-1])]

    def dot(a, b):
        total = a[0] * b[0]
        for x in range(1, cx):
            total = total + a[x] * b[x]
        return jnp.sum(total, axis=0, keepdims=True)

    def coarse_apply(p):
        product = []
        for x in range(cx):
            v = diag[x] * p[x] - north[x] * pltpu.roll(p[x], cy - 1, 0) - south[x] * pltpu.roll(p[x], 1, 0)
            if x < cx - 1:
                v = v - east[x] * p[x + 1]
            if x > 0:
                v = v - east[x - 1] * p[x - 1]
            product.append(v)
        return product

    def iterate_once(counter, carried):
        estimate, remainder, search, norm_now = carried
        product = coarse_apply(search)
        alpha = norm_now / dot(search, product)
        estimate = [e + alpha * s for e, s in zip(estimate, search)]
        remainder = [r - alpha * q for r, q in zip(remainder, product)]
        norm_next = dot(remainder, remainder)
        beta = norm_next / norm_now
        search = [r + beta * s for r, s in zip(remainder, search)]
        return estimate, remainder, search, norm_next

    state = ([jnp.zeros((cy, 128), jnp.float32)] * cx, coarse_source, coarse_source,
             dot(coarse_source, coarse_source))
    estimate = lax.fori_loop(0, CG_ITERS, iterate_once, state)[0]
    for x in range(cx):
        E[x] = estimate[x]

    ring = lax.broadcasted_iota(jnp.int32, (Y, 128), 0)

    def share(dx):
        def one(dy):
            jx, jy = ix + dx, iy + dy
            row = E[jnp.clip(jx, 0, cx - 1), pl.ds(jnp.clip(jy, 0, cy - 1), 1), :]
            keep = inside(jx, jy, cx, cy).astype(jnp.float32)
            return jnp.broadcast_to(row * keep, (Y, 128))
        return jnp.where(ring < ny, one(0), jnp.where(ring < ny + H, one(1), one(-1)))

    shares = {dx: share(dx) for dx in (-1, 0, 1)}

    for d in range(8):
        each(d, -1, lambda d=d: halo2(d).wait_recv())
    for d in range(8):
        each(d, 1, lambda d=d: halo2(d).wait_send())

    def edge(x, dx):
        V[x, ny:ny + H, :] = YHI2[x]
        V[x, ny + H:Y, :] = YLO2[x]
        V[x] = V[x] + shares[dx]

    for i in range(NU):
        V[1 + i, 0:ny, :] = XLO2[i]
        V[X - H + i, 0:ny, :] = XHI2[i]
    for i in range(NU):
        edge(1 + i, -1)
        edge(X - H + i, 1)

    def middle(x, c):
        edge(x, 0)
        return c

    rows_loop(H, H + nx, middle, 0)

    sweep(V, U, 2, X - 2)
    sweep(U, V, 3, X - 3)
    sweep(V, U, 4, X - 4)
    back = pltpu.make_async_copy(U.at[H:H + nx, 0:ny, :], out, osem)
    back.start()

    for d in range(8):
        def sent(d=d):
            for a in range(3):
                halo(a, d).wait_send()
        each(d, 1, sent)
    run(coef_x, cx, "wait_send")
    run(coef_y, cy, "wait_send")
    run(sum_x, cx, "wait_send")
    run(sum_y, cy, "wait_send")
    back.wait()


def body(conductivity, source, initial):
    nx, ny, nz = conductivity.shape
    cx, cy = lax.axis_size("gx"), lax.axis_size("gy")
    X, Y = nx + 2 * H, ny + 2 * H
    args = (conductivity, source, initial)
    thin = tuple(a.reshape(nx, ny, 1, nz) for a in args)
    wide = pltpu.VMEM((X, Y, nz), jnp.float32)
    dma = pltpu.SemaphoreType.DMA

    def vmem(*shape):
        return pltpu.VMEM(shape, jnp.float32)

    return pl.pallas_call(
        functools.partial(kernel, cx, cy, nx, ny),
        out_shape=jax.ShapeDtypeStruct((nx, ny, nz), jnp.float32),
        in_specs=[pl.BlockSpec(memory_space=pltpu.HBM)] * 6,
        out_specs=pl.BlockSpec(memory_space=pl.ANY),
        scratch_shapes=[wide] * 9 + [
            *[vmem(X, w, 1, nz) for w in WIDTH + WIDTH],
            vmem(NU, ny, nz), vmem(NU, ny, nz), vmem(X, H, nz), vmem(X, H, nz),
            vmem(nx, H, nz), vmem(nx, H, nz),
            vmem(cy, cx, 1, nz), vmem(cy, cx, 1, nz), vmem(cx, cy, nz), vmem(2, cx, cy, nz),
            dma((3,)), dma,
            dma((24,)), dma((24,)), dma((8,)), dma((8,)),
            dma((cx - 1,)), dma((cx - 1,)), dma((cy - 1,)), dma((cy - 1,)),
            dma((cx - 1,)), dma((cx - 1,)), dma((cy - 1,)), dma((cy - 1,)),
        ],
        compiler_params=pltpu.CompilerParams(collective_id=0, has_side_effects=True),
        name="cycle",
    )(*args, *thin)


def solution(mesh):
    return jax.shard_map(
        body,
        mesh=mesh,
        in_specs=(P("gx", "gy", None), P("gx", "gy", None), P("gx", "gy", None)),
        out_specs=P("gx", "gy", None),
        check_vma=False,
    )
```

```python
import functools

import jax
import jax.numpy as jnp
from jax import lax
from jax.experimental import pallas as pl
from jax.experimental.pallas import tpu as pltpu
from jax.sharding import PartitionSpec as P

NU = 3
CG_ITERS = 32
H = NU + 1
WIDTH = (NU, NU - 1, NU)

relax_weight = 0.8
MESH = pl.DeviceIdType.MESH
DIRS = [(1, 0), (-1, 0), (0, 1), (0, -1), (1, 1), (1, -1), (-1, 1), (-1, -1)]


def inside(ix, iy, cx, cy):
    return (ix >= 0) & (ix < cx) & (iy >= 0) & (iy < cy)


def rows_loop(lo, hi, step, carry):
    count = hi - lo
    pairs = count // 2

    def two(i, c):
        x = lo + 2 * i
        return step(x + 1, step(x, c))

    carry = lax.fori_loop(0, pairs, two, carry)
    if count % 2:
        carry = step(hi - 1, carry)
    return carry


ROWS = 8
DIRECT = 64


def blocks_loop(lo, hi, block, carry):
    count = (hi - lo) // ROWS
    carry = lax.fori_loop(0, count, lambda i, c: block(lo + ROWS * i, c, ROWS), carry)
    if (hi - lo) % ROWS:
        carry = block(lo + ROWS * count, carry, (hi - lo) % ROWS)
    return carry


def kernel(cx, cy, nx, ny, *refs):
    (k_in, f_in, u_in, k1, f1, u1, out,
     K, F, U, V, CE, CN, CU, CD, W, YLO_K, YLO_F, YLO_U, YHI_K, YHI_F, YHI_U,
     XLO2, XHI2, YLO2, YHI2, PLO, PHI, GC, GS, E, R,
     lsem, osem, ssem, rsem, ssem2, rsem2,
     c1s, c1r, c2s, c2r, s1s, s1r, s2s, s2r, das, dar) = refs
    X = nx + 2 * H
    Y = ny + 2 * H
    ix = lax.axis_index("gx")
    iy = lax.axis_index("gy")
    full = [k_in, f_in, u_in]
    thin = [k1, f1, u1]
    ext = [K, F, U]
    YLO = [YLO_K, YLO_F, YLO_U]
    YHI = [YHI_K, YHI_F, YHI_U]

    barrier = pltpu.get_barrier_semaphore()

    def greet_x(k, c):
        pl.semaphore_signal(barrier, inc=1, device_id=(lax.rem(ix + k, cx), iy), device_id_type=MESH)
        return c

    def greet_y(k, c):
        pl.semaphore_signal(barrier, inc=1, device_id=(ix, lax.rem(iy + k, cy)), device_id_type=MESH)
        return c

    lax.fori_loop(1, cx, greet_x, 0)
    lax.fori_loop(1, cy, greet_y, 0)
    for dx, dy in DIRS[4:]:
        @pl.when(inside(ix + dx, iy + dy, cx, cy))
        def _(dx=dx, dy=dy):
            pl.semaphore_signal(barrier, inc=1, device_id=(ix + dx, iy + dy), device_id_type=MESH)

    local = [pltpu.make_async_copy(full[a], ext[a].at[H:H + nx, 0:ny, :], lsem.at[a]) for a in range(3)]
    for copy in local:
        copy.start()

    sides_x = (ix > 0).astype(jnp.int32) + (ix < cx - 1).astype(jnp.int32)
    sides_y = (iy > 0).astype(jnp.int32) + (iy < cy - 1).astype(jnp.int32)
    pl.semaphore_wait(barrier, (cx - 1) + (cy - 1) + sides_x * sides_y)

    def spans(dx, w):
        src = {1: (nx - w, nx), -1: (0, w), 0: (0, nx)}[dx]
        dst = {1: (H - w, H), -1: (X - H, X - H + w), 0: (H, H + nx)}[dx]
        return src, dst

    def halo(a, d):
        dx, dy = DIRS[d]
        slot = a * 8 + d
        w = WIDTH[a]
        src_rows, dst_rows = spans(dx, w)
        if dy == 0:
            src = full[a].at[src_rows[0]:src_rows[1]]
            dst = ext[a].at[dst_rows[0]:dst_rows[1], 0:ny, :]
        else:
            cols = (ny - w, ny) if dy == 1 else (0, w)
            src = thin[a].at[src_rows[0]:src_rows[1], cols[0]:cols[1]]
            dst = (YLO if dy == 1 else YHI)[a].at[dst_rows[0]:dst_rows[1]]
        return pltpu.make_async_remote_copy(
            src_ref=src, dst_ref=dst, send_sem=ssem.at[slot], recv_sem=rsem.at[slot],
            device_id=(ix + dx, iy + dy), device_id_type=MESH)

    def each(d, sign, act):
        dx, dy = DIRS[d]
        pl.when(inside(ix + sign * dx, iy + sign * dy, cx, cy))(act)

    for d in range(8):
        def start(d=d):
            for a in range(3):
                halo(a, d).start()
        each(d, 1, start)

    def clear_when_absent(d):
        dx, dy = DIRS[d]

        @pl.when(jnp.logical_not(inside(ix - dx, iy - dy, cx, cy)))
        def _():
            for a in range(3):
                w = WIDTH[a]
                lo, hi = spans(dx, w)[1]
                if dy == 0:
                    ext[a][lo:hi, 0:ny, :] = jnp.zeros((w, ny, 128), jnp.float32)
                else:
                    (YLO if dy == 1 else YHI)[a][lo:hi] = jnp.zeros((hi - lo, w, 1, 128), jnp.float32)
            if dy == 0:
                (XLO2 if dx == 1 else XHI2)[...] = jnp.zeros((NU, ny, 128), jnp.float32)
            else:
                lo, hi = spans(dx, H)[1]
                (YLO2 if dy == 1 else YHI2)[lo:hi] = jnp.zeros((hi - lo, H, 128), jnp.float32)

    for d in range(8):
        clear_when_absent(d)

    for copy in local:
        copy.wait()

    def along_x(G, ss, rs):
        def of(k):
            return pltpu.make_async_remote_copy(
                src_ref=G.at[iy, ix], dst_ref=G.at[iy, ix], send_sem=ss.at[k - 1], recv_sem=rs.at[k - 1],
                device_id=(lax.rem(ix + k, cx), iy), device_id_type=MESH)
        return of

    def along_y(G, ss, rs):
        def of(k):
            return pltpu.make_async_remote_copy(
                src_ref=G.at[iy], dst_ref=G.at[iy], send_sem=ss.at[k - 1], recv_sem=rs.at[k - 1],
                device_id=(ix, lax.rem(iy + k, cy)), device_id_type=MESH)
        return of

    def to_all(k):
        target = lax.rem(ix * cy + iy + k, cx * cy)
        return pltpu.make_async_remote_copy(
            src_ref=GS.at[iy, ix], dst_ref=GS.at[iy, ix], send_sem=das.at[k - 1], recv_sem=dar.at[k - 1],
            device_id=(target // cy, lax.rem(target, cy)), device_id_type=MESH)

    direct = cx * cy <= DIRECT

    def run(of, count, method):
        def go(k, c):
            getattr(of(k), method)()
            return c
        lax.fori_loop(1, count, go, 0)

    coef_x, coef_y = along_x(GC, c1s, c1r), along_y(GC, c2s, c2r)
    sum_x, sum_y = along_x(GS, s1s, s1r), along_y(GS, s2s, s2r)

    lane_row = lax.broadcasted_iota(jnp.int32, (1, 128), 1)

    def whole(v):
        return jnp.sum(jnp.sum(v, axis=0, keepdims=True), axis=1, keepdims=True)

    def in_lanes(values):
        row = jnp.zeros((1, 128), jnp.float32)
        for k, v in enumerate(values):
            row = jnp.where(lane_row == k, v, row)
        return row

    def outer(x, c):
        return c[0] + K[x, 0:1, :], c[1] + K[x, ny - 1:ny, :]

    none = jnp.zeros((1, 128), jnp.float32)
    y_first, y_last = rows_loop(H, H + nx, outer, (none, none))
    GC[iy, ix] = in_lanes([whole(K[H, 0:ny, :]), whole(K[H + nx - 1, 0:ny, :]), whole(y_first), whole(y_last)])
    run(coef_x, cx, "start")
    f_total = rows_loop(H, H + nx, lambda x, c: c + F[x, 0:ny, :], jnp.zeros((ny, 128), jnp.float32))
    f_total = jnp.sum(f_total, axis=0, keepdims=True)

    run(coef_x, cx, "wait_recv")
    run(coef_y, cy, "start")

    for d in range(8):
        def finish(d=d):
            for a in range(3):
                halo(a, d).wait_recv()
        each(d, -1, finish)

    def unpack(x, c):
        for a in range(3):
            w = WIDTH[a]
            ext[a][x, ny:ny + w, :] = YHI[a][x, :, 0, :]
            ext[a][x, Y - w:Y, :] = YLO[a][x, :, 0, :]
        return c

    rows_loop(1, X - 1, unpack, 0)

    lane = lax.broadcasted_iota(jnp.int32, (Y, 128), 1)
    up_half = jnp.where(lane < 127, 0.5, 0.0)
    down_half = jnp.where(lane > 0, 0.5, 0.0)

    def next_y(v):
        return pltpu.roll(v, Y - 1, 0)

    def last_y(v):
        return pltpu.roll(v, 1, 0)

    def next_z(v):
        return pltpu.roll(v, 127, 1)

    def last_z(v):
        return pltpu.roll(v, 1, 1)

    def faces(x, c, rows):
        k, west = c
        ks = [k] + [K[x + 1 + r] for r in range(rows)]
        ups = [next_z(ks[r]) for r in range(rows)]
        downs = [last_z(ks[r]) for r in range(rows)]
        for r in range(rows):
            k = ks[r]
            east = 0.5 * (k + ks[r + 1])
            north = 0.5 * (k + next_y(k))
            up = up_half * (k + ups[r])
            down = down_half * (k + downs[r])
            d = east + west + north + last_y(north) + up + down
            CE[x + r] = east
            CN[x + r] = north
            CU[x + r] = up
            CD[x + r] = down
            W[x + r] = jnp.where(k > 0, relax_weight / jnp.where(k > 0, d, 1.0), 0.0)
            west = east
        return ks[rows], west

    zero = jnp.zeros((Y, 128), jnp.float32)
    CE[1] = 0.5 * (K[1] + K[2])
    blocks_loop(2, X - 2, faces, (K[2], CE[1]))

    def sweep(src, dst, lo, hi, final=False):
        def block(x, c, rows):
            u, west, low, high = c
            us = [u] + [src[x + 1 + r] for r in range(rows)]
            ups = [next_z(us[r]) for r in range(rows)]
            downs = [last_z(us[r]) for r in range(rows)]
            for r in range(rows):
                u = us[r]
                east = CE[x + r] * (us[r + 1] - u)
                cn = CN[x + r]
                north = cn * (next_y(u) - u)
                change = ((east - west) + (north - last_y(north))
                          + (CU[x + r] * (ups[r] - u) + CD[x + r] * (downs[r] - u)))
                new = u + W[x + r] * (F[x + r] + change)
                dst[x + r] = new
                if final:
                    low, high = low + cn[Y - 1:Y] * new[0:1], high + cn[ny - 1:ny] * new[ny - 1:ny]
                west = east
            return us[rows], west, low, high

        start = (src[lo], CE[lo - 1] * (src[lo] - src[lo - 1]))
        start += (none, none) if final else (0, 0)
        return blocks_loop(lo, hi, block, start)[2:]

    sweep(U, V, 2, X - 2)
    sweep(V, U, 3, X - 3)
    y_low, y_high = sweep(U, V, 4, X - 4, True)

    x_low = jnp.sum(CE[H - 1, 0:ny, :] * V[H, 0:ny, :], axis=0, keepdims=True)
    x_high = jnp.sum(CE[X - H - 1, 0:ny, :] * V[X - H - 1, 0:ny, :], axis=0, keepdims=True)
    own = f_total - x_low - x_high - y_low - y_high
    GS[iy, ix] = in_lanes([jnp.sum(v, axis=1, keepdims=True) for v in (own, x_low, x_high, y_low, y_high)])
    if direct:
        run(coef_y, cy, "wait_recv")
        run(to_all, cx * cy, "start")
    else:
        run(sum_x, cx, "start")
        run(coef_y, cy, "wait_recv")

    def pack(x, c):
        PLO[x] = V[H + x, 0:H, :]
        PHI[x] = V[H + x, ny - H:ny, :]
        return c

    rows_loop(0, nx, pack, 0)

    def halo2(d):
        dx, dy = DIRS[d]
        src_rows = {1: (nx - H, nx), -1: (0, H), 0: (0, nx)}[dx]
        dst_rows = {1: (0, H), -1: (X - H, X), 0: (H, H + nx)}[dx]
        if dy == 0:
            src = V.at[nx + 1:nx + H, 0:ny, :] if dx == 1 else V.at[H:H + NU, 0:ny, :]
            dst = XLO2 if dx == 1 else XHI2
        else:
            src = (PHI if dy == 1 else PLO).at[src_rows[0]:src_rows[1]]
            dst = (YLO2 if dy == 1 else YHI2).at[dst_rows[0]:dst_rows[1]]
        return pltpu.make_async_remote_copy(
            src_ref=src, dst_ref=dst, send_sem=ssem2.at[d], recv_sem=rsem2.at[d],
            device_id=(ix + dx, iy + dy), device_id_type=MESH)

    row_y = lax.broadcasted_iota(jnp.int32, (cy, 128), 0)

    def tidy(G, k):
        for x in range(cx):
            for y in range(cy):
                R[k, x, y:y + 1, :] = G[y, x]
        return [R[k, x] for x in range(cx)]

    def lane_of(rows, k):
        return [jnp.broadcast_to(r[:, k:k + 1], (cy, 128)) for r in rows]

    def after_y(v):
        return jnp.where(row_y < cy - 1, pltpu.roll(v, cy - 1, 0), 0.0)

    def before_y(v):
        return jnp.where(row_y > 0, pltpu.roll(v, 1, 0), 0.0)

    coarse_rows = tidy(GC, 0)
    nil = jnp.zeros((cy, 128), jnp.float32)
    x_first, x_last, y_first, y_last = [lane_of(coarse_rows, k) for k in range(4)]
    east = [0.5 * (a + b) for a, b in zip(x_last, x_first[1:] + [nil])]
    west = [0.5 * (a + b) for a, b in zip(x_first, [nil] + x_last[:-1])]
    north = [0.5 * (a + after_y(b)) for a, b in zip(y_last, y_first)]
    south = [0.5 * (a + before_y(b)) for a, b in zip(y_first, y_last)]
    diag = [a + b + c + d for a, b, c, d in zip(east, west, north, south)]
    north = [jnp.where(row_y < cy - 1, n, 0.0) for n in north]
    south = [pltpu.roll(n, 1, 0) for n in north]

    if not direct:
        run(sum_x, cx, "wait_recv")
        run(sum_y, cy, "start")
    for d in range(8):
        each(d, 1, lambda d=d: halo2(d).start())
    run(*((to_all, cx * cy) if direct else (sum_y, cy)), "wait_recv")
    coarse_rows = tidy(GS, 1)
    own, x_low, x_high, y_low, y_high = [lane_of(coarse_rows, k) for k in range(5)]
    coarse_source = [
        (a + after_y(b)) + (before_y(c) + d + e)
        for a, b, c, d, e in zip(own, y_low, y_high, x_low[1:] + [nil], [nil] + x_high[:-1])]

    def dot(a, b):
        total = a[0] * b[0]
        for x in range(1, cx):
            total = total + a[x] * b[x]
        return jnp.sum(total, axis=0, keepdims=True)

    def coarse_apply(p):
        product = []
        for x in range(cx):
            v = diag[x] * p[x] - north[x] * pltpu.roll(p[x], cy - 1, 0) - south[x] * pltpu.roll(p[x], 1, 0)
            if x < cx - 1:
                v = v - east[x] * p[x + 1]
            if x > 0:
                v = v - east[x - 1] * p[x - 1]
            product.append(v)
        return product

    def iterate_once(counter, carried):
        estimate, remainder, search, norm_now = carried
        product = coarse_apply(search)
        alpha = norm_now / dot(search, product)
        estimate = [e + alpha * s for e, s in zip(estimate, search)]
        remainder = [r - alpha * q for r, q in zip(remainder, product)]
        norm_next = dot(remainder, remainder)
        beta = norm_next / norm_now
        search = [r + beta * s for r, s in zip(remainder, search)]
        return estimate, remainder, search, norm_next

    state = ([jnp.zeros((cy, 128), jnp.float32)] * cx, coarse_source, coarse_source,
             dot(coarse_source, coarse_source))
    estimate = lax.fori_loop(0, CG_ITERS, iterate_once, state)[0]
    for x in range(cx):
        E[x] = estimate[x]

    ring = lax.broadcasted_iota(jnp.int32, (Y, 128), 0)

    def share(dx):
        def one(dy):
            jx, jy = ix + dx, iy + dy
            row = E[jnp.clip(jx, 0, cx - 1), pl.ds(jnp.clip(jy, 0, cy - 1), 1), :]
            keep = inside(jx, jy, cx, cy).astype(jnp.float32)
            return jnp.broadcast_to(row * keep, (Y, 128))
        return jnp.where(ring < ny, one(0), jnp.where(ring < ny + H, one(1), one(-1)))

    shares = {dx: share(dx) for dx in (-1, 0, 1)}

    for d in range(8):
        each(d, -1, lambda d=d: halo2(d).wait_recv())
    for d in range(8):
        each(d, 1, lambda d=d: halo2(d).wait_send())

    def edge(x, dx):
        V[x, ny:ny + H, :] = YHI2[x]
        V[x, ny + H:Y, :] = YLO2[x]
        V[x] = V[x] + shares[dx]

    for i in range(NU):
        V[1 + i, 0:ny, :] = XLO2[i]
        V[X - H + i, 0:ny, :] = XHI2[i]
    for i in range(NU):
        edge(1 + i, -1)
        edge(X - H + i, 1)

    def middle(x, c):
        edge(x, 0)
        return c

    rows_loop(H, H + nx, middle, 0)

    sweep(V, U, 2, X - 2)
    sweep(U, V, 3, X - 3)
    half = nx // 2
    back = [pltpu.make_async_copy(U.at[H + r:H + r + half, 0:ny, :], out.at[r:r + half], osem.at[i])
            for i, r in enumerate((0, half))]
    sweep(V, U, H, H + half)
    back[0].start()
    sweep(V, U, H + half, H + nx)
    back[1].start()

    for d in range(8):
        def sent(d=d):
            for a in range(3):
                halo(a, d).wait_send()
        each(d, 1, sent)
    run(coef_x, cx, "wait_send")
    run(coef_y, cy, "wait_send")
    if direct:
        run(to_all, cx * cy, "wait_send")
    else:
        run(sum_x, cx, "wait_send")
        run(sum_y, cy, "wait_send")
    for copy in back:
        copy.wait()


def body(conductivity, source, initial):
    nx, ny, nz = conductivity.shape
    cx, cy = lax.axis_size("gx"), lax.axis_size("gy")
    X, Y = nx + 2 * H, ny + 2 * H
    args = (conductivity, source, initial)
    thin = tuple(a.reshape(nx, ny, 1, nz) for a in args)
    wide = pltpu.VMEM((X, Y, nz), jnp.float32)
    dma = pltpu.SemaphoreType.DMA

    def vmem(*shape):
        return pltpu.VMEM(shape, jnp.float32)

    return pl.pallas_call(
        functools.partial(kernel, cx, cy, nx, ny),
        out_shape=jax.ShapeDtypeStruct((nx, ny, nz), jnp.float32),
        in_specs=[pl.BlockSpec(memory_space=pltpu.HBM)] * 6,
        out_specs=pl.BlockSpec(memory_space=pl.ANY),
        scratch_shapes=[wide] * 9 + [
            *[vmem(X, w, 1, nz) for w in WIDTH + WIDTH],
            vmem(NU, ny, nz), vmem(NU, ny, nz), vmem(X, H, nz), vmem(X, H, nz),
            vmem(nx, H, nz), vmem(nx, H, nz),
            vmem(cy, cx, 1, nz), vmem(cy, cx, 1, nz), vmem(cx, cy, nz), vmem(2, cx, cy, nz),
            dma((3,)), dma((2,)),
            dma((24,)), dma((24,)), dma((8,)), dma((8,)),
            dma((cx - 1,)), dma((cx - 1,)), dma((cy - 1,)), dma((cy - 1,)),
            dma((cx - 1,)), dma((cx - 1,)), dma((cy - 1,)), dma((cy - 1,)),
            dma((min(cx * cy, DIRECT) - 1,)), dma((min(cx * cy, DIRECT) - 1,)),
        ],
        compiler_params=pltpu.CompilerParams(collective_id=0, has_side_effects=True),
        name="cycle",
    )(*args, *thin)


def solution(mesh):
    return jax.shard_map(
        body,
        mesh=mesh,
        in_specs=(P("gx", "gy", None), P("gx", "gy", None), P("gx", "gy", None)),
        out_specs=P("gx", "gy", None),
        check_vma=False,
    )
```
